32 devices in a mesh: dp: 16 (over z, x, core), tensor: 2 (over y).
Axes of the slice: x: 2, y: 2, z: 4, core: 2. Of those that a mesh axis runs over, the one named last changes fastest.
Arguments:
- hidden_in: bfloat16 [16384, 1024], P(('dp', 'tensor')), may hold values from -6 to 6
- positions: int32 [16384], P('dp'), may hold values from 0 to 1023, as said below
- gain_attention: float32 [1024], replicated, may hold values from 0.1 to 1.9
- gain_feedforward: float32 [1024], replicated, may hold values from 0.1 to 1.9
- gain_query: float32 [128], replicated, may hold values from 0.7 to 5
- gain_key: float32 [128], replicated, may hold values from 0.7 to 5
- query_proj: bfloat16 [1024, 2048], P('dp', 'tensor'), may hold values from -0.1875 to 0.1875
- key_proj: bfloat16 [1024, 1024], P('dp', 'tensor'), may hold values from -0.1875 to 0.1875
- value_proj: bfloat16 [1024, 1024], P('dp', 'tensor'), may hold values from -0.1875 to 0.1875
- out_proj: bfloat16 [2048, 1024], P(('tensor', 'dp')), may hold values from -3 to 3
- gate_proj: bfloat16 [1024, 3072], P('dp', 'tensor'), may hold values from -0.1875 to 0.1875
- up_proj: bfloat16 [1024, 3072], P('dp', 'tensor'), may hold values from -0.1875 to 0.1875
- down_proj: bfloat16 [3072, 1024], P(('tensor', 'dp')), may hold values from -0.21875 to 0.21875
- cotangent: bfloat16 [16384, 1024], P(('dp', 'tensor')), may hold values from -6 to 6
Outputs:
- hidden_out: bfloat16 [16384, 1024], P(('dp', 'tensor'))
- grad_hidden: float32 [16384, 1024], P(('dp', 'tensor'))
- attention_gain_grad: float32 [1024], replicated
- feedforward_gain_grad: float32 [1024], replicated
- query_gain_grad: float32 [128], replicated
- key_gain_grad: float32 [128], replicated
- query_grads: float32 [1024, 2048], P('dp', 'tensor')
- key_grads: float32 [1024, 1024], P('dp', 'tensor')
- value_grads: float32 [1024, 1024], P('dp', 'tensor')
- out_grads: float32 [2048, 1024], P(('tensor', 'dp'))
- gate_grads: float32 [1024, 3072], P('dp', 'tensor')
- up_grads: float32 [1024, 3072], P('dp', 'tensor')
- down_grads: float32 [3072, 1024], P(('tensor', 'dp'))
The draws below stay inside these ranges and needn't reach their ends.
Inputs may be any that keep to these rules, and one draw needn't show every extreme that they name: Within each sequence of 1024 tokens the positions start at 0 and rise by one from token to token, except that they restart at 0 where a document begins; some sequence holds one document.
All inputs are finite; a program needn't handle non-finite values.
Results may differ from the reference program's by a relative error of at most 0.02.
The reference program's roundings to bfloat16 on the way (of `normed_attn`, `probs_b`, `heads_b`, `normed_mlp`, `active_b` and `grad_scores_b`) count: a program that leaves them out, or rounds other values in their place, can miss the bound.
Values may be sent and summed in bfloat16 or wider, within the bound.
No kernel may reach another device: no remote copies, remote signals or barrier semaphores. Data moves between devices by JAX's collectives and lax.ppermute only.
A program may use at most 256 MiB of HBM per device.

```python
import math
import jax
import jax.numpy as jnp
from jax import lax

D = 1024
H = 16
KV = 8
HD = 128
FF = 3072
LEN = 1024
TOKENS = 16384
N_DP = 16


def draw_positions(key, part):
    seq_count = TOKENS // LEN
    mark_key = jax.random.fold_in(key, 11)
    pick_key = jax.random.fold_in(key, 12)
    token_index = jnp.arange(LEN, dtype=jnp.int32)[None, :]
    doc_starts = jax.random.randint(mark_key, (seq_count, LEN), 0, 48) == 0
    single = jax.random.randint(pick_key, (), 0, seq_count)
    seq_index = jnp.arange(seq_count, dtype=jnp.int32)[:, None]
    doc_starts = doc_starts & (seq_index != single) | (token_index == 0)
    starts = lax.cummax(jnp.where(doc_starts, token_index, 0), axis=1)
    return (token_index - starts).reshape(TOKENS).astype(jnp.int32)


def head_gain(key, salt):
    gain_key = jax.random.fold_in(key, salt)
    return jnp.exp(jax.random.uniform(gain_key, (HD,), jnp.float32, -0.35, 0.35))


def draw_gain_query(key, part):
    return head_gain(key, 21)


def draw_gain_key(key, part):
    return head_gain(key, 22)


def strengthened(drawn, own_key, source, target, shards_of, factor):
    owner, partner = [(jnp.arange(drawn.shape[position]) // (drawn.shape[position] // shards_of)).reshape([-1 if axis == position else 1 for axis in range(drawn.ndim)]) for position in (source, target)]
    chosen = jax.random.permutation(own_key, shards_of)[partner]
    strong = (owner == chosen) | (owner == (partner + shards_of // 2) % shards_of)
    return jnp.where(strong, factor * drawn, drawn)


def level_of(stream_key, dims, cuts, smallest, largest):
    def one(dim, shards_of):
        draws = jax.random.uniform(jax.random.fold_in(jax.random.fold_in(stream_key, 6), dim), (shards_of,), jnp.float32, smallest / len(cuts), largest / len(cuts))
        return jnp.repeat(jnp.exp(draws), dims[dim] // shards_of).reshape((-1,) + (1,) * (len(dims) - dim - 1))

    level = one(*cuts[0])
    for cut in cuts[1:]:
        level = level * one(*cut)
    return level


def bell_draw(rng, extent, scale, bound, shards=(), kind=jnp.bfloat16):
    values = scale * jax.random.normal(rng, extent, jnp.float32)
    if shards:
        values = values * level_of(rng, extent, shards, -0.22, 0.18)
    return jnp.clip(values, -bound, bound).astype(kind)


def noise_with(rng, shape, spread, limit, pieces, heavy, kind=jnp.bfloat16):
    values = spread * jax.random.normal(rng, shape, jnp.float32)
    if pieces:
        values = values * level_of(rng, shape, pieces, -0.22, 0.18)
    return jnp.clip(strengthened(values, jax.random.fold_in(rng, 3), *heavy), -limit, limit).astype(kind)


def setup_inputs(seed: int = 0) -> dict:
    seeds = jax.random.split(jax.random.key(seed), 15)
    return {
        "hidden_in": noise_with(seeds[0], (TOKENS, D), 1.0, 6.0, ((0, 32),), (0, 1, 32, 2.75)),
        "positions": draw_positions(jax.random.fold_in(seeds[14], 71), 0),
        "gain_attention": jnp.clip(1.0 + 0.18 * jax.random.normal(seeds[2], (D,), jnp.float32), 0.1, 1.9),
        "gain_feedforward": jnp.clip(1.0 + 0.18 * jax.random.normal(seeds[3], (D,), jnp.float32), 0.1, 1.9),
        "gain_query": draw_gain_query(jax.random.fold_in(seeds[14], 71), 0),
        "gain_key": draw_gain_key(jax.random.fold_in(seeds[14], 71), 0),
        "query_proj": bell_draw(seeds[6], (D, H * HD), D ** -0.5, 0.1875, ((0, 16), (1, 2))),
        "key_proj": bell_draw(seeds[7], (D, KV * HD), D ** -0.5, 0.1875, ((0, 16), (1, 2))),
        "value_proj": bell_draw(seeds[8], (D, KV * HD), D ** -0.5, 0.1875, ((0, 16), (1, 2))),
        "out_proj": bell_draw(seeds[9], (H * HD, D), (2 * H * HD // LEN) ** -0.5, 3.0, ((0, 32),)),
        "gate_proj": bell_draw(seeds[10], (D, FF), D ** -0.5, 0.1875, ((0, 16), (1, 2))),
        "up_proj": bell_draw(seeds[11], (D, FF), D ** -0.5, 0.1875, ((0, 16), (1, 2))),
        "down_proj": bell_draw(seeds[12], (FF, D), (FF // 4) ** -0.5, 0.21875, ((0, 32),)),
        "cotangent": bell_draw(seeds[13], (TOKENS, D), 1.0, 6.0, ((0, 32),)),
    }


EPS = 1e-06
THETA = 1000000.0

def rotary_tables(positions, width):
    half_width = width // 2
    freq_index = jnp.arange(half_width).astype(jnp.float32)
    inverse_freq = jnp.exp(freq_index * (-2.0 * math.log(THETA) / width))
    angles = positions.astype(jnp.float32)[:, None] * inverse_freq[None, :]
    return (jnp.cos(angles)[:, None, :], jnp.sin(angles)[:, None, :])

def rotate(values, cosine_table, sine_table):
    half_width = values.shape[-1] // 2
    lower_half = values[..., :half_width]
    upper_half = values[..., half_width:]
    return jnp.concatenate((lower_half * cosine_table - upper_half * sine_table, upper_half * cosine_table + lower_half * sine_table), -1)

def rotate_back(grad_values, cosine_table, sine_table):
    half_width = grad_values.shape[-1] // 2
    lower_half = grad_values[..., :half_width]
    upper_half = grad_values[..., half_width:]
    return jnp.concatenate((lower_half * cosine_table + upper_half * sine_table, upper_half * cosine_table - lower_half * sine_table), -1)

def rms_unit(values):
    inv_scale = lax.rsqrt(lax.optimization_barrier(jnp.mean(values * values, -1, keepdims=True)) + EPS)
    return (values * inv_scale, inv_scale)

def rms_back(grad_out, gain_vec, unit_vals, inv_scale):
    scaled_grad = grad_out * gain_vec
    return inv_scale * (scaled_grad - unit_vals * lax.optimization_barrier(jnp.mean(scaled_grad * unit_vals, -1, keepdims=True)))

def attend(query_b, key_b, value_b):
    length = query_b.shape[0]
    block_rows = min(length, 512)
    block_count = length // block_rows
    scale_qk = 1.0 / math.sqrt(query_b.shape[-1])
    key_f = key_b.astype(jnp.float32)
    value_f = value_b.astype(jnp.float32)
    outputs = []
    log_sums = []
    for block in range(block_count):
        row_start = block * block_rows
        key_end = row_start + block_rows
        query_block = query_b[row_start:key_end].astype(jnp.float32)
        scores = jnp.einsum('qgrd,kgd->grqk', query_block, key_f[:key_end]) * scale_qk
        causal = (row_start + jnp.arange(block_rows, dtype=jnp.int32))[:, None] >= jnp.arange(key_end, dtype=jnp.int32)[None, :]
        scores = jnp.where(causal, scores, -jnp.inf)
        top_score = lax.optimization_barrier(jnp.max(scores, -1, keepdims=True))
        shifted = jnp.exp(scores - top_score)
        sum_exp = lax.optimization_barrier(jnp.sum(shifted, -1, keepdims=True))
        probs_b = (shifted / sum_exp).astype(jnp.bfloat16)
        outputs.append(jnp.einsum('grqk,kgd->qgrd', probs_b.astype(jnp.float32), value_f[:key_end]))
        log_sums.append(top_score + jnp.log(sum_exp))
    return (jnp.concatenate(outputs, 0), log_sums)

def attend_back(query_b, key_b, value_b, grad_b, log_sums):
    length = query_b.shape[0]
    block_rows = min(length, 512)
    block_count = length // block_rows
    scale_qk = 1.0 / math.sqrt(query_b.shape[-1])
    key_f = key_b.astype(jnp.float32)
    value_f = value_b.astype(jnp.float32)
    key_acc = jnp.zeros(key_b.shape, jnp.float32)
    value_acc = jnp.zeros(key_b.shape, jnp.float32)
    grad_queries = []
    for block in range(block_count):
        row_start = block * block_rows
        key_end = row_start + block_rows
        query_f = query_b[row_start:key_end].astype(jnp.float32)
        grad_f = grad_b[row_start:key_end].astype(jnp.float32)
        scores = jnp.einsum('qgrd,kgd->grqk', query_f, key_f[:key_end]) * scale_qk
        causal = (row_start + jnp.arange(block_rows, dtype=jnp.int32))[:, None] >= jnp.arange(key_end, dtype=jnp.int32)[None, :]
        scores = jnp.where(causal, scores, -jnp.inf)
        probs = jnp.exp(scores - log_sums[block])
        probs_b = probs.astype(jnp.bfloat16)
        grad_probs = jnp.einsum('qgrd,kgd->grqk', grad_f, value_f[:key_end])
        row_dot = lax.optimization_barrier(jnp.sum(probs * grad_probs, -1, keepdims=True))
        grad_scores_b = (probs * (grad_probs - row_dot)).astype(jnp.bfloat16)
        grad_scores_f = grad_scores_b.astype(jnp.float32)
        grad_queries.append(jnp.einsum('grqk,kgd->qgrd', grad_scores_f, key_f[:key_end]) * scale_qk)
        key_acc = key_acc.at[:key_end].add(jnp.einsum('grqk,qgrd->kgd', grad_scores_f, query_f) * scale_qk)
        value_acc = value_acc.at[:key_end].add(jnp.einsum('grqk,qgrd->kgd', probs_b.astype(jnp.float32), grad_f))
    return (jnp.concatenate(grad_queries, 0), key_acc, value_acc)

def layer_sequence(hidden_seq, position_seq, cot_seq, gains, mats):
    gain_attn, gain_mlp, gain_q, gain_k = gains
    proj_qkv, proj_out, proj_gate, proj_up, proj_down = mats
    length = hidden_seq.shape[0]
    width_query = H * HD
    width_key = KV * HD
    cosine_table, sine_table = rotary_tables(position_seq, HD)
    hidden_f = hidden_seq.astype(jnp.float32)
    unit_attn, scale_attn = rms_unit(hidden_f)
    normed_attn = (unit_attn * gain_attn).astype(jnp.bfloat16)
    projected = jnp.dot(normed_attn, proj_qkv, preferred_element_type=jnp.float32)
    query_raw = projected[:, :width_query].reshape(length, H, HD)
    key_raw = projected[:, width_query:width_query + width_key].reshape(length, KV, HD)
    value_b = projected[:, width_query + width_key:].astype(jnp.bfloat16).reshape(length, KV, HD)
    query_unit, query_scale = rms_unit(query_raw)
    key_unit, key_scale = rms_unit(key_raw)
    query_b = rotate(query_unit * gain_q, cosine_table, sine_table).astype(jnp.bfloat16).reshape(length, KV, H // KV, HD)
    key_b = rotate(key_unit * gain_k, cosine_table, sine_table).astype(jnp.bfloat16)
    heads_out, log_sums = attend(query_b, key_b, value_b)
    heads_b = heads_out.reshape(length, width_query).astype(jnp.bfloat16)
    resid = hidden_f + jnp.dot(heads_b, proj_out, preferred_element_type=jnp.float32)
    unit_mlp, scale_mlp = rms_unit(resid)
    normed_mlp = (unit_mlp * gain_mlp).astype(jnp.bfloat16)
    gate_val = jnp.dot(normed_mlp, proj_gate, preferred_element_type=jnp.float32)
    up_val = jnp.dot(normed_mlp, proj_up, preferred_element_type=jnp.float32)
    sigmoid_gate = jax.nn.sigmoid(gate_val)
    active_b = (gate_val * sigmoid_gate * up_val).astype(jnp.bfloat16)
    output_b = (resid + jnp.dot(active_b, proj_down, preferred_element_type=jnp.float32)).astype(jnp.bfloat16)
    grad_down = jnp.dot(active_b.T, cot_seq, preferred_element_type=jnp.float32)
    grad_active = jnp.dot(cot_seq, proj_down.T, preferred_element_type=jnp.float32)
    grad_gate_b = (grad_active * up_val * sigmoid_gate * (1.0 + gate_val * (1.0 - sigmoid_gate))).astype(jnp.bfloat16)
    grad_up_b = (grad_active * gate_val * sigmoid_gate).astype(jnp.bfloat16)
    grad_gate = jnp.dot(normed_mlp.T, grad_gate_b, preferred_element_type=jnp.float32)
    grad_up = jnp.dot(normed_mlp.T, grad_up_b, preferred_element_type=jnp.float32)
    grad_normed_mlp = jnp.dot(grad_gate_b, proj_gate.T, preferred_element_type=jnp.float32) + jnp.dot(grad_up_b, proj_up.T, preferred_element_type=jnp.float32)
    term_mlp = lax.optimization_barrier(jnp.sum(grad_normed_mlp * unit_mlp, 0))
    grad_resid = cot_seq.astype(jnp.float32) + rms_back(grad_normed_mlp, gain_mlp, unit_mlp, scale_mlp)
    grad_resid_b = grad_resid.astype(jnp.bfloat16)
    grad_out = jnp.dot(heads_b.T, grad_resid_b, preferred_element_type=jnp.float32)
    grad_heads_b = jnp.dot(grad_resid_b, proj_out.T, preferred_element_type=jnp.float32).astype(jnp.bfloat16).reshape(length, KV, H // KV, HD)
    grad_qrot, grad_krot, grad_value = attend_back(query_b, key_b, value_b, grad_heads_b, log_sums)
    grad_qnormed = rotate_back(grad_qrot.reshape(length, H, HD), cosine_table, sine_table)
    grad_knormed = rotate_back(grad_krot, cosine_table, sine_table)
    term_query = lax.optimization_barrier(jnp.sum(grad_qnormed * query_unit, (0, 1)))
    term_key = lax.optimization_barrier(jnp.sum(grad_knormed * key_unit, (0, 1)))
    grad_qkv_b = jnp.concatenate((rms_back(grad_qnormed, gain_q, query_unit, query_scale).reshape(length, width_query), rms_back(grad_knormed, gain_k, key_unit, key_scale).reshape(length, width_key), grad_value.reshape(length, width_key)), 1).astype(jnp.bfloat16)
    grad_qkv = jnp.dot(normed_attn.T, grad_qkv_b, preferred_element_type=jnp.float32)
    grad_normed_attn = jnp.dot(grad_qkv_b, proj_qkv.T, preferred_element_type=jnp.float32)
    term_attn = lax.optimization_barrier(jnp.sum(grad_normed_attn * unit_attn, 0))
    grad_hidden = grad_resid + rms_back(grad_normed_attn, gain_attn, unit_attn, scale_attn)
    return (output_b, grad_hidden, (term_attn, term_mlp, term_query, term_key, grad_qkv, grad_out, grad_gate, grad_up, grad_down))

def reference(hidden_in, positions, gain_attention, gain_feedforward, gain_query, gain_key, query_proj, key_proj, value_proj, out_proj, gate_proj, up_proj, down_proj, cotangent):
    proj_qkv = jnp.concatenate((query_proj, key_proj, value_proj), 1)
    gains = (gain_attention, gain_feedforward, gain_query, gain_key)
    mats = (proj_qkv, out_proj, gate_proj, up_proj, down_proj)
    hidden_seqs = hidden_in.reshape(N_DP, LEN, D)
    position_seqs = positions.reshape(N_DP, LEN)
    cot_seqs = cotangent.reshape(N_DP, LEN, D)
    initial = (jnp.zeros((D,), jnp.float32), jnp.zeros((D,), jnp.float32), jnp.zeros((HD,), jnp.float32), jnp.zeros((HD,), jnp.float32), jnp.zeros(proj_qkv.shape, jnp.float32), jnp.zeros(out_proj.shape, jnp.float32), jnp.zeros(gate_proj.shape, jnp.float32), jnp.zeros(up_proj.shape, jnp.float32), jnp.zeros(down_proj.shape, jnp.float32))

    def one_sequence(carried, inputs):
        hidden_seq, position_seq, cot_seq = inputs
        output_b, grad_hidden, terms = layer_sequence(hidden_seq, position_seq, cot_seq, gains, mats)
        carried = jax.tree.map(lambda left, right: left + right, carried, terms)
        return (carried, (output_b, grad_hidden))
    totals, (outputs, grad_inputs) = lax.scan(one_sequence, initial, (hidden_seqs, position_seqs, cot_seqs))
    term_attn, term_mlp, term_query, term_key, grad_qkv, grad_out, grad_gate, grad_up, grad_down = totals
    width_query = H * HD
    width_key = KV * HD
    return (outputs.reshape(TOKENS, D), grad_inputs.reshape(TOKENS, D), term_attn, term_mlp, term_query, term_key, grad_qkv[:, :width_query], grad_qkv[:, width_query:width_query + width_key], grad_qkv[:, width_query + width_key:], grad_out, grad_gate, grad_up, grad_down)
```

```python
import math

import jax
import jax.numpy as jnp
from jax import lax
from jax.sharding import PartitionSpec as P

HD = 128
EPS = 1e-06
THETA = 1000000.0
BF = jnp.bfloat16
F32 = jnp.float32


def rotary_tables(positions, width):
    half_width = width // 2
    freq_index = jnp.arange(half_width).astype(F32)
    inverse_freq = jnp.exp(freq_index * (-2.0 * math.log(THETA) / width))
    angles = positions.astype(F32)[:, None] * inverse_freq[None, :]
    return (jnp.cos(angles)[:, None, :], jnp.sin(angles)[:, None, :])


def rotate(values, cosine_table, sine_table):
    half_width = values.shape[-1] // 2
    lower_half = values[..., :half_width]
    upper_half = values[..., half_width:]
    return jnp.concatenate(
        (
            lower_half * cosine_table - upper_half * sine_table,
            upper_half * cosine_table + lower_half * sine_table,
        ),
        -1,
    )


def rms_unit(values):
    inv_scale = lax.rsqrt(jnp.mean(values * values, -1, keepdims=True) + EPS)
    return (values * inv_scale, inv_scale)


def rms_back(grad_out, gain_vec, unit_vals, inv_scale):
    scaled_grad = grad_out * gain_vec
    return inv_scale * (
        scaled_grad - unit_vals * jnp.mean(scaled_grad * unit_vals, -1, keepdims=True)
    )


def matmul(left, right):
    return jnp.dot(left, right, preferred_element_type=F32)


def contract_rows(left, right):
    return lax.dot_general(left, right, (((0,), (0,)), ((), ())), preferred_element_type=F32)


def contract_cols(left, right):
    return lax.dot_general(left, right, (((1,), (1,)), ((), ())), preferred_element_type=F32)


def attend(query_b, key_b, value_b):
    length = query_b.shape[0]
    block_rows = min(length, 512)
    block_count = length // block_rows
    scale_qk = 1.0 / math.sqrt(query_b.shape[-1])
    outputs = []
    log_sums = []
    for block in range(block_count):
        row_start = block * block_rows
        key_end = row_start + block_rows
        query_block = query_b[row_start:key_end]
        scores = (
            jnp.einsum(
                "qgrd,kgd->grqk", query_block, key_b[:key_end], preferred_element_type=F32
            )
            * scale_qk
        )
        causal = (row_start + jnp.arange(block_rows, dtype=jnp.int32))[:, None] >= jnp.arange(
            key_end, dtype=jnp.int32
        )[None, :]
        scores = jnp.where(causal, scores, -jnp.inf)
        top_score = jnp.max(scores, -1, keepdims=True)
        shifted = jnp.exp(scores - top_score)
        sum_exp = jnp.sum(shifted, -1, keepdims=True)
        probs_b = (shifted / sum_exp).astype(BF)
        outputs.append(
            jnp.einsum("grqk,kgd->qgrd", probs_b, value_b[:key_end], preferred_element_type=F32)
        )
        log_sums.append(top_score + jnp.log(sum_exp))
    return (jnp.concatenate(outputs, 0), log_sums)


def attend_back(query_b, key_b, value_b, grad_b, log_sums):
    length = query_b.shape[0]
    block_rows = min(length, 512)
    block_count = length // block_rows
    scale_qk = 1.0 / math.sqrt(query_b.shape[-1])
    key_acc = jnp.zeros(key_b.shape, F32)
    value_acc = jnp.zeros(key_b.shape, F32)
    grad_queries = []
    for block in range(block_count):
        row_start = block * block_rows
        key_end = row_start + block_rows
        query_block = query_b[row_start:key_end]
        grad_block = grad_b[row_start:key_end]
        keys_seen = key_b[:key_end]
        scores = (
            jnp.einsum("qgrd,kgd->grqk", query_block, keys_seen, preferred_element_type=F32)
            * scale_qk
        )
        causal = (row_start + jnp.arange(block_rows, dtype=jnp.int32))[:, None] >= jnp.arange(
            key_end, dtype=jnp.int32
        )[None, :]
        scores = jnp.where(causal, scores, -jnp.inf)
        probs = jnp.exp(scores - log_sums[block])
        probs_b = probs.astype(BF)
        grad_probs = jnp.einsum(
            "qgrd,kgd->grqk", grad_block, value_b[:key_end], preferred_element_type=F32
        )
        row_dot = jnp.sum(probs * grad_probs, -1, keepdims=True)
        grad_scores_b = (probs * (grad_probs - row_dot)).astype(BF)
        grad_queries.append(
            jnp.einsum("grqk,kgd->qgrd", grad_scores_b, keys_seen, preferred_element_type=F32)
            * scale_qk
        )
        key_acc = key_acc.at[:key_end].add(
            jnp.einsum("grqk,qgrd->kgd", grad_scores_b, query_block, preferred_element_type=F32)
            * scale_qk
        )
        value_acc = value_acc.at[:key_end].add(
            jnp.einsum("grqk,qgrd->kgd", probs_b, grad_block, preferred_element_type=F32)
        )
    return (jnp.concatenate(grad_queries, 0), key_acc, value_acc)


def all_sum(value, sizes):
    for axis, size in sizes:
        if size & (size - 1):
            value = lax.psum(value, axis)
            continue
        step = 1
        while step < size:
            value = value + lax.ppermute(value, axis, [(i, i ^ step) for i in range(size)])
            step *= 2
    return value


def make_local(n_dp, n_tensor):
    paired = n_tensor == 2
    swap = [(0, 1), (1, 0)]

    def gather_rows(own):
        if paired:
            return jnp.concatenate((own, lax.ppermute(own, "tensor", swap)), 0)
        return lax.all_gather(own, "tensor", axis=0, tiled=True)

    def to_sequence(rows):
        if not paired:
            return rows
        half = rows.shape[0] // 2
        first = lax.axis_index("tensor") == 0
        return jnp.concatenate(
            (
                jnp.where(first, rows[:half], rows[half:]),
                jnp.where(first, rows[half:], rows[:half]),
            ),
            0,
        )

    def scatter_rows(part, operand):
        if paired:
            half = operand[0].shape[0] // 2
            sent = part(*(o[half:] for o in operand)).astype(BF)
            got = lax.ppermute(sent, "tensor", swap)
            return part(*(o[:half] for o in operand)) + got.astype(F32)
        return lax.psum_scatter(
            part(*operand).astype(BF), "tensor", scatter_dimension=0, tiled=True
        ).astype(F32)

    def local(
        hidden_in,
        positions,
        gain_attention,
        gain_feedforward,
        gain_query,
        gain_key,
        query_proj,
        key_proj,
        value_proj,
        out_proj,
        gate_proj,
        up_proj,
        down_proj,
        cotangent,
    ):
        length = positions.shape[0]
        own = hidden_in.shape[0]
        width = hidden_in.shape[1]
        heads_here = query_proj.shape[1] // HD
        groups_here = key_proj.shape[1] // HD
        width_query = heads_here * HD
        width_key = groups_here * HD
        width_qkv = width_query + 2 * width_key
        units = gate_proj.shape[1]
        shard_rows = query_proj.shape[0]

        shard_attn = jnp.concatenate(
            (query_proj, key_proj, value_proj, out_proj.reshape(shard_rows, -1)), 1
        )
        shard_mlp = jnp.concatenate((gate_proj, up_proj, down_proj.reshape(shard_rows, -1)), 1)
        full_attn = lax.all_gather(shard_attn, "dp", axis=0, tiled=True)
        full_mlp = lax.all_gather(shard_mlp, "dp", axis=0, tiled=True)
        proj_qkv = full_attn[:, :width_qkv]
        full_out = full_attn[:, width_qkv:].reshape(-1, width)
        full_gateup = full_mlp[:, : 2 * units]
        full_down = full_mlp[:, 2 * units :].reshape(-1, width)

        rows_hidden = gather_rows(hidden_in)
        rows_cot = gather_rows(cotangent)
        cosine_table, sine_table = rotary_tables(positions, HD)
        unit_rows, scale_rows = rms_unit(rows_hidden.astype(F32))
        rows_attn = (unit_rows * gain_attention).astype(BF)
        if paired:
            hidden_f, unit_attn, scale_attn = (
                hidden_in.astype(F32),
                unit_rows[:own],
                scale_rows[:own],
            )
        else:
            hidden_f = hidden_in.astype(F32)
            unit_attn, scale_attn = rms_unit(hidden_f)

        projected = to_sequence(matmul(rows_attn, proj_qkv))
        query_raw = projected[:, :width_query].reshape(length, heads_here, HD)
        key_raw = projected[:, width_query : width_query + width_key].reshape(
            length, groups_here, HD
        )
        value_b = (
            projected[:, width_query + width_key :].astype(BF).reshape(length, groups_here, HD)
        )
        query_unit, query_scale = rms_unit(query_raw)
        key_unit, key_scale = rms_unit(key_raw)
        query_b = (
            rotate(query_unit * gain_query, cosine_table, sine_table)
            .astype(BF)
            .reshape(length, groups_here, heads_here // groups_here, HD)
        )
        key_b = rotate(key_unit * gain_key, cosine_table, sine_table).astype(BF)
        heads_out, log_sums = attend(query_b, key_b, value_b)
        heads_b = to_sequence(heads_out.reshape(length, width_query).astype(BF))
        resid = hidden_f + scatter_rows(lambda h: matmul(h, full_out), (heads_b,))
        unit_mlp, scale_mlp = rms_unit(resid)
        rows_mlp = gather_rows((unit_mlp * gain_feedforward).astype(BF))
        gate_val = matmul(rows_mlp, full_gateup[:, :units])
        up_val = matmul(rows_mlp, full_gateup[:, units:])
        sigmoid_gate = jax.nn.sigmoid(gate_val)
        active_b = (gate_val * sigmoid_gate * up_val).astype(BF)
        output_b = (resid + scatter_rows(lambda a: matmul(a, full_down), (active_b,))).astype(BF)

        grad_active = contract_cols(rows_cot, full_down)
        grad_gate_b = (
            grad_active * up_val * sigmoid_gate * (1.0 + gate_val * (1.0 - sigmoid_gate))
        ).astype(BF)
        grad_up_b = (grad_active * gate_val * sigmoid_gate).astype(BF)
        grad_normed_mlp = scatter_rows(
            lambda g, u: contract_cols(g, full_gateup[:, :units])
            + contract_cols(u, full_gateup[:, units:]),
            (grad_gate_b, grad_up_b),
        )
        grad_mlp_w = jnp.concatenate(
            (
                contract_rows(rows_mlp, grad_gate_b).astype(BF),
                contract_rows(rows_mlp, grad_up_b).astype(BF),
                contract_rows(active_b, rows_cot).astype(BF).reshape(width, -1),
            ),
            1,
        )
        sent_mlp = lax.psum_scatter(grad_mlp_w, "dp", scatter_dimension=0, tiled=True)

        term_feedforward = jnp.sum(grad_normed_mlp * unit_mlp, 0)
        grad_resid = cotangent.astype(F32) + rms_back(
            grad_normed_mlp, gain_feedforward, unit_mlp, scale_mlp
        )
        rows_resid = gather_rows(grad_resid.astype(BF))
        grad_heads_b = (
            to_sequence(contract_cols(rows_resid, full_out).astype(BF))
            .reshape(length, groups_here, heads_here // groups_here, HD)
        )
        grad_qrot, grad_krot, grad_value = attend_back(
            query_b, key_b, value_b, grad_heads_b, log_sums
        )
        grad_qnormed = rotate(
            grad_qrot.reshape(length, heads_here, HD), cosine_table, -sine_table
        )
        grad_knormed = rotate(grad_krot, cosine_table, -sine_table)
        term_query = jnp.sum(grad_qnormed * query_unit, (0, 1))
        term_key = jnp.sum(grad_knormed * key_unit, (0, 1))
        grad_qkv_b = to_sequence(
            jnp.concatenate(
                (
                    rms_back(grad_qnormed, gain_query, query_unit, query_scale).reshape(
                        length, width_query
                    ),
                    rms_back(grad_knormed, gain_key, key_unit, key_scale).reshape(
                        length, width_key
                    ),
                    grad_value.reshape(length, width_key),
                ),
                1,
            ).astype(BF)
        )
        grad_attn_w = jnp.concatenate(
            (
                contract_rows(rows_attn, grad_qkv_b).astype(BF),
                contract_rows(heads_b, rows_resid).astype(BF).reshape(width, -1),
            ),
            1,
        )
        sent_attn = lax.psum_scatter(grad_attn_w, "dp", scatter_dimension=0, tiled=True)
        grad_normed_attn = scatter_rows(lambda g: contract_cols(g, proj_qkv), (grad_qkv_b,))
        term_attention = jnp.sum(grad_normed_attn * unit_attn, 0)
        grad_hidden = grad_resid + rms_back(
            grad_normed_attn, gain_attention, unit_attn, scale_attn
        )
        terms = all_sum(
            jnp.concatenate((term_attention, term_feedforward, term_query, term_key)).reshape(
                -1, HD
            ),
            (("tensor", n_tensor), ("dp", n_dp)),
        ).reshape(-1)
        sent_attn = sent_attn.astype(F32)
        sent_mlp = sent_mlp.astype(F32)
        return (
            output_b,
            grad_hidden,
            terms[:width],
            terms[width : 2 * width],
            terms[2 * width : 2 * width + HD],
            terms[2 * width + HD :],
            sent_attn[:, :width_query],
            sent_attn[:, width_query : width_query + width_key],
            sent_attn[:, width_query + width_key : width_qkv],
            sent_attn[:, width_qkv:].reshape(out_proj.shape),
            sent_mlp[:, :units],
            sent_mlp[:, units : 2 * units],
            sent_mlp[:, 2 * units :].reshape(down_proj.shape),
        )

    return local


def solution(mesh):
    rows = P(("dp", "tensor"), None)
    cut = P("dp", "tensor")
    stacked = P(("tensor", "dp"), None)
    return jax.shard_map(
        make_local(mesh.shape["dp"], mesh.shape["tensor"]),
        mesh=mesh,
        in_specs=(
            rows,
            P("dp"),
            P(),
            P(),
            P(),
            P(),
            cut,
            cut,
            cut,
            stacked,
            cut,
            cut,
            stacked,
            rows,
        ),
        out_specs=(rows, rows, P(), P(), P(), P(), cut, cut, cut, stacked, cut, cut, stacked),
        check_vma=False,
    )
```

```python
import functools
import math

import jax
import jax.numpy as jnp
from jax import lax
from jax.experimental import pallas as pl
from jax.experimental.pallas import tpu as pltpu
from jax.sharding import PartitionSpec as P

HD = 128
EPS = 1e-06
THETA = 1000000.0
BF = jnp.bfloat16
F32 = jnp.float32


def rotary_tables(positions, width):
    half_width = width // 2
    freq_index = jnp.arange(half_width).astype(F32)
    inverse_freq = jnp.exp(freq_index * (-2.0 * math.log(THETA) / width))
    angles = positions.astype(F32)[:, None] * inverse_freq[None, :]
    cosine, sine = jnp.cos(angles), jnp.sin(angles)
    return jnp.concatenate((cosine, cosine), 1), jnp.concatenate((-sine, sine), 1)


def rms_unit(values):
    inv_scale = lax.rsqrt(jnp.mean(values * values, -1, keepdims=True) + EPS)
    return (values * inv_scale, inv_scale)


def rms_back(grad_out, gain_vec, unit_vals, inv_scale):
    scaled_grad = grad_out * gain_vec
    return inv_scale * (
        scaled_grad - unit_vals * jnp.mean(scaled_grad * unit_vals, -1, keepdims=True)
    )


def matmul(left, right):
    return jnp.dot(left, right, preferred_element_type=F32)


def contract_rows(left, right):
    return lax.dot_general(left, right, (((0,), (0,)), ((), ())), preferred_element_type=F32)


def contract_cols(left, right):
    return lax.dot_general(left, right, (((1,), (1,)), ((), ())), preferred_element_type=F32)


BLOCK = 256


def turn(values, cosine, sine):
    return values * cosine + pltpu.roll(values, HD // 2, 1) * sine


def turn_back(values, cosine, sine):
    return values * cosine - pltpu.roll(values, HD // 2, 1) * sine


def unit_of(raw):
    inv_scale = lax.rsqrt(jnp.mean(raw * raw, -1, keepdims=True) + EPS)
    return raw * inv_scale, inv_scale


def heads_stacked(ref, rows, per_group):
    return jnp.concatenate([ref[rows, r * HD : (r + 1) * HD] for r in range(per_group)], 0)


def causal_mask(key_end, row_start, block, per_group):
    keys = lax.broadcasted_iota(jnp.int32, (key_end, per_group * block), 0)
    queries = lax.broadcasted_iota(jnp.int32, (key_end, per_group * block), 1)
    return keys <= row_start + (queries & (block - 1))


def attend_kernel(
    x_ref,
    wq_ref,
    wk_ref,
    wv_ref,
    cos_ref,
    sin_ref,
    gq_ref,
    gk_ref,
    heads_ref,
    qraw_ref,
    kraw_ref,
    qb_ref,
    kb_ref,
    vb_ref,
    lse_ref,
    *,
    per_group,
    block,
):
    length = x_ref.shape[0]
    scale_qk = 1.0 / math.sqrt(HD)
    for i in range(length // block):
        rows = slice(i * block, (i + 1) * block)
        x = x_ref[rows, :]
        cosine, sine = cos_ref[rows, :], sin_ref[rows, :]
        qraw = jnp.dot(x, wq_ref[...], preferred_element_type=F32)
        kraw = jnp.dot(x, wk_ref[...], preferred_element_type=F32)
        qraw_ref[rows, :] = qraw
        kraw_ref[rows, :] = kraw
        vb_ref[rows, :] = jnp.dot(x, wv_ref[...], preferred_element_type=F32).astype(BF)
        for r in range(per_group):
            cols = slice(r * HD, (r + 1) * HD)
            unit, _ = unit_of(qraw[:, cols])
            qb_ref[rows, cols] = turn(unit * gq_ref[...], cosine, sine).astype(BF)
        unit, _ = unit_of(kraw)
        kb_ref[rows, :] = turn(unit * gk_ref[...], cosine, sine).astype(BF)
        key_end = (i + 1) * block
        queries = heads_stacked(qb_ref, rows, per_group)
        scores = contract_cols(kb_ref[:key_end, :], queries) * scale_qk
        scores = jnp.where(causal_mask(key_end, i * block, block, per_group), scores, -jnp.inf)
        top = jnp.max(scores, 0, keepdims=True)
        shifted = jnp.exp(scores - top)
        total = jnp.sum(shifted, 0, keepdims=True)
        probs = (shifted * (1.0 / total)).astype(BF)
        out = contract_rows(vb_ref[:key_end, :], probs).T
        log_sum = top + jnp.log(total)
        for r in range(per_group):
            part = slice(r * block, (r + 1) * block)
            heads_ref[rows, r * HD : (r + 1) * HD] = out[part, :].astype(BF)
            lse_ref[r : r + 1, rows] = log_sum[:, part]


def attend_back_kernel(
    resid_ref,
    wo_ref,
    qb_ref,
    kb_ref,
    vb_ref,
    qraw_ref,
    kraw_ref,
    lse_ref,
    cos_ref,
    sin_ref,
    gq_ref,
    gk_ref,
    grad_ref,
    term_ref,
    key_acc,
    value_acc,
    *,
    per_group,
    block,
    groups,
):
    length = resid_ref.shape[0]
    scale_qk = 1.0 / math.sqrt(HD)
    group = pl.program_id(0)
    blocks = length // block

    @pl.when(group == 0)
    def _():
        term_ref[...] = jnp.zeros_like(term_ref)

    def column(index):
        return pl.ds(pl.multiple_of(index * HD, HD), HD)

    for i in reversed(range(blocks)):
        rows = slice(i * block, (i + 1) * block)
        key_end = (i + 1) * block
        grad = contract_cols(resid_ref[rows, :], wo_ref[...]).astype(BF)
        grads = jnp.concatenate(
            [grad[:, r * HD : (r + 1) * HD] for r in range(per_group)], 0
        )
        queries = heads_stacked(qb_ref, rows, per_group)
        keys, values = kb_ref[:key_end, :], vb_ref[:key_end, :]
        log_sum = jnp.concatenate([lse_ref[r : r + 1, rows] for r in range(per_group)], 1)
        scores = contract_cols(keys, queries) * scale_qk
        probs = jnp.where(
            causal_mask(key_end, i * block, block, per_group), jnp.exp(scores - log_sum), 0.0
        )
        grad_probs = contract_cols(values, grads)
        row_dot = jnp.sum(probs * grad_probs, 0, keepdims=True)
        grad_scores = (probs * (grad_probs - row_dot)).astype(BF)
        value_part = jnp.dot(probs.astype(BF), grads, preferred_element_type=F32)
        key_part = jnp.dot(grad_scores, queries, preferred_element_type=F32) * scale_qk
        if i == blocks - 1:
            value_acc[...] = value_part
            key_acc[...] = key_part
        else:
            value_acc[:key_end, :] += value_part
            key_acc[:key_end, :] += key_part
        grad_query = contract_rows(keys, grad_scores).T * scale_qk
        cosine, sine = cos_ref[rows, :], sin_ref[rows, :]
        for r in range(per_group):
            normed = turn_back(grad_query[r * block : (r + 1) * block, :], cosine, sine)
            unit, inv_scale = unit_of(qraw_ref[rows, r * HD : (r + 1) * HD])
            term_ref[0:1, :] += jnp.sum(normed * unit, 0, keepdims=True)
            grad_ref[rows, column(group * per_group + r)] = rms_back(
                normed, gq_ref[...], unit, inv_scale
            ).astype(BF)
    for i in range(blocks):
        rows = slice(i * block, (i + 1) * block)
        normed = turn_back(key_acc[rows, :], cos_ref[rows, :], sin_ref[rows, :])
        unit, inv_scale = unit_of(kraw_ref[rows, :])
        term_ref[1:2, :] += jnp.sum(normed * unit, 0, keepdims=True)
        grad_ref[rows, column(groups * per_group + group)] = rms_back(
            normed, gk_ref[...], unit, inv_scale
        ).astype(BF)
        grad_ref[rows, column(groups * (per_group + 1) + group)] = value_acc[rows, :].astype(BF)


def attend(rows_attn, full_attn, tables, gains, groups, per_group):
    length, width = rows_attn.shape
    block = min(length, BLOCK)
    heads = groups * per_group
    whole = lambda shape: pl.BlockSpec(shape, lambda g: (0, 0))
    wide = pl.BlockSpec((length, per_group * HD), lambda g: (0, g))
    narrow = pl.BlockSpec((length, HD), lambda g: (0, g))
    return pl.pallas_call(
        functools.partial(attend_kernel, per_group=per_group, block=block),
        name="attend",
        grid=(groups,),
        in_specs=[
            whole((length, width)),
            pl.BlockSpec((width, per_group * HD), lambda g: (0, g)),
            pl.BlockSpec((width, HD), lambda g: (0, heads + g)),
            pl.BlockSpec((width, HD), lambda g: (0, heads + groups + g)),
            whole((length, HD)),
            whole((length, HD)),
            whole((1, HD)),
            whole((1, HD)),
        ],
        out_specs=[
            wide,
            wide,
            narrow,
            wide,
            narrow,
            narrow,
            pl.BlockSpec((None, per_group, length), lambda g: (g, 0, 0)),
        ],
        out_shape=[
            jax.ShapeDtypeStruct((length, heads * HD), BF),
            jax.ShapeDtypeStruct((length, heads * HD), F32),
            jax.ShapeDtypeStruct((length, groups * HD), F32),
            jax.ShapeDtypeStruct((length, heads * HD), BF),
            jax.ShapeDtypeStruct((length, groups * HD), BF),
            jax.ShapeDtypeStruct((length, groups * HD), BF),
            jax.ShapeDtypeStruct((groups, per_group, length), F32),
        ],
        cost_estimate=pl.CostEstimate(
            flops=2 * length * width * (heads + 2 * groups) * HD + 3 * length * length * heads * HD,
            bytes_accessed=length * (heads + 2 * groups) * HD * 10,
            transcendentals=length * length * heads,
        ),
    )(rows_attn, full_attn, full_attn, full_attn, *tables, *gains)


def attend_back(rows_resid, full_out, out_column, saved, tables, gains, groups, per_group):
    length, width = rows_resid.shape
    qraw, kraw, qb, kb, vb, lse = saved
    block = min(length, BLOCK)
    heads = groups * per_group
    columns = (heads + 2 * groups) * HD
    whole = lambda shape: pl.BlockSpec(shape, lambda g: (0, 0))
    wide = pl.BlockSpec((length, per_group * HD), lambda g: (0, g))
    narrow = pl.BlockSpec((length, HD), lambda g: (0, g))
    return pl.pallas_call(
        functools.partial(attend_back_kernel, per_group=per_group, block=block, groups=groups),
        name="attend_back",
        grid=(groups,),
        in_specs=[
            whole((length, width)),
            pl.BlockSpec((per_group * HD, width), lambda g: (g, out_column)),
            wide,
            narrow,
            narrow,
            wide,
            narrow,
            pl.BlockSpec((None, per_group, length), lambda g: (g, 0, 0)),
            whole((length, HD)),
            whole((length, HD)),
            whole((1, HD)),
            whole((1, HD)),
        ],
        out_specs=[whole((length, columns)), whole((8, HD))],
        out_shape=[
            jax.ShapeDtypeStruct((length, columns), BF),
            jax.ShapeDtypeStruct((8, HD), F32),
        ],
        scratch_shapes=[pltpu.VMEM((length, HD), F32), pltpu.VMEM((length, HD), F32)],
        cost_estimate=pl.CostEstimate(
            flops=2 * length * width * heads * HD + 7 * length * length * heads * HD,
            bytes_accessed=length * columns * 10,
            transcendentals=length * length * heads,
        ),
    )(rows_resid, full_out, qb, kb, vb, qraw, kraw, lse, *tables, *gains)


def mlp_kernel(
    x_ref,
    cot_ref,
    wg_ref,
    wu_ref,
    wd_ref,
    *refs,
    steps,
):
    active_ref, gate_ref, up_ref, down_ref, normed_ref, down_acc, normed_acc = refs[-7:]
    step = pl.program_id(0)

    @pl.when(step == 0)
    def _():
        down_acc[...] = jnp.zeros_like(down_acc)
        normed_acc[...] = jnp.zeros_like(normed_acc)

    half = min(x_ref.shape[0], 256)
    for i in range(x_ref.shape[0] // half):
        rows = slice(i * half, (i + 1) * half)
        x = x_ref[rows, :]
        gate = jnp.dot(x, wg_ref[...], preferred_element_type=F32)
        up = jnp.dot(x, wu_ref[...], preferred_element_type=F32)
        grad_active = contract_cols(cot_ref[rows, :], wd_ref[...])
        sigmoid = 1.0 / (1.0 + jnp.exp(-gate))
        silu = gate * sigmoid
        active = (silu * up).astype(BF)
        grad_gate = (grad_active * up * sigmoid * (1.0 + gate * (1.0 - sigmoid))).astype(BF)
        grad_up = (grad_active * silu).astype(BF)
        active_ref[rows, :] = active
        gate_ref[rows, :] = grad_gate
        up_ref[rows, :] = grad_up
        down_acc[rows, :] += jnp.dot(active, wd_ref[...], preferred_element_type=F32)
        normed_acc[rows, :] += contract_cols(grad_gate, wg_ref[...]) + contract_cols(
            grad_up, wu_ref[...]
        )

    @pl.when(step == steps - 1)
    def _():
        down_ref[...] = down_acc[...].astype(down_ref.dtype)
        normed_ref[...] = normed_acc[...].astype(normed_ref.dtype)


def mlp(rows_x, rows_cot, part, parts, full_mlp, full_down, units, dtype, held=()):
    rows, width = rows_x.shape
    block = next(b for b in (384, 256, 128) if units % b == 0)
    steps = units // block
    whole = pl.BlockSpec((rows, width), lambda j: (0, 0))
    piece = pl.BlockSpec((rows, block), lambda j: (part, j))
    full = jax.ShapeDtypeStruct((rows * parts, units), BF)
    total = jax.ShapeDtypeStruct((rows, width), dtype)
    return pl.pallas_call(
        functools.partial(mlp_kernel, steps=steps),
        name="feed_forward",
        grid=(steps,),
        in_specs=[
            whole,
            whole,
            pl.BlockSpec((width, block), lambda j: (0, j)),
            pl.BlockSpec((width, block), lambda j: (0, steps + j)),
            pl.BlockSpec((block, width), lambda j: (j, 0)),
        ]
        + [pl.BlockSpec(memory_space=pl.ANY)] * len(held),
        out_specs=[piece, piece, piece, whole, whole],
        out_shape=[full, full, full, total, total],
        input_output_aliases={5 + i: i for i in range(len(held))},
        scratch_shapes=[pltpu.VMEM((rows, width), F32), pltpu.VMEM((rows, width), F32)],
        cost_estimate=pl.CostEstimate(
            flops=12 * rows * width * units,
            bytes_accessed=6 * width * units + 6 * rows * units,
            transcendentals=rows * units,
        ),
    )(rows_x, rows_cot, full_mlp, full_mlp, full_down, *held)


def all_sum(value, sizes):
    for axis, size in sizes:
        if size & (size - 1):
            value = lax.psum(value, axis)
            continue
        step = 1
        while step < size:
            value = value + lax.ppermute(value, axis, [(i, i ^ step) for i in range(size)])
            step *= 2
    return value


def pack_rows(shard, rows):
    count, width = shard.shape
    if 2 * count == 3 * rows and rows % 32 == 0:
        tail = shard[rows:]
        half = width // 2
        return jnp.concatenate(
            (shard[:rows], jnp.concatenate((tail[:, :half], tail[:, half:]), 0)), 1
        )
    return shard.reshape(rows, -1)


def unpack_rows(packed, parts, width):
    total, wide = packed.shape
    rows = total // parts
    if 2 * wide == 3 * width and rows % 32 == 0:
        blocks = packed.reshape(parts, rows, wide)
        tail = blocks[:, :, width:]
        tail = jnp.concatenate((tail[:, : rows // 2], tail[:, rows // 2 :]), 2)
        return jnp.concatenate((blocks[:, :, :width], tail), 1).reshape(-1, width)
    return packed.reshape(-1, width)


def pack_blocks(full, parts, rows):
    total, width = full.shape
    count = total // parts
    if 2 * count == 3 * rows and rows % 32 == 0:
        blocks = full.reshape(parts, count, width)
        tail = blocks[:, rows:]
        half = width // 2
        tail = jnp.concatenate((tail[:, :, :half], tail[:, :, half:]), 1)
        return jnp.concatenate((blocks[:, :rows], tail), 2).reshape(parts * rows, -1)
    return full.reshape(parts * rows, -1)


def make_local(n_dp, n_tensor):
    paired = n_tensor == 2

    def swap(value):
        return lax.ppermute(value, "tensor", [(0, 1), (1, 0)])

    def in_order(own, other):
        first = lax.axis_index("tensor") == 0
        return jnp.concatenate((jnp.where(first, own, other), jnp.where(first, other, own)), 0)

    def sequence_rows(own):
        if paired:
            return in_order(own, swap(own))
        return lax.all_gather(own, "tensor", axis=0, tiled=True)

    def scatter_rows(part, operand):
        if paired:
            half = operand.shape[0] // 2
            me = lax.axis_index("tensor")
            other_rows = lax.dynamic_slice_in_dim(operand, (1 - me) * half, half, 0)
            own_rows = lax.dynamic_slice_in_dim(operand, me * half, half, 0)
            got = swap(part(other_rows).astype(BF))
            return part(own_rows) + got.astype(F32)
        return sum_rows(part(operand).astype(BF))

    def sum_rows(value):
        return lax.psum_scatter(value, "tensor", scatter_dimension=0, tiled=True).astype(F32)

    def local(
        hidden_in,
        positions,
        gain_attention,
        gain_feedforward,
        gain_query,
        gain_key,
        query_proj,
        key_proj,
        value_proj,
        out_proj,
        gate_proj,
        up_proj,
        down_proj,
        cotangent,
    ):
        width = hidden_in.shape[1]
        heads_here = query_proj.shape[1] // HD
        groups_here = key_proj.shape[1] // HD
        per_group = heads_here // groups_here
        width_query = heads_here * HD
        width_key = groups_here * HD
        width_qkv = width_query + 2 * width_key
        units = gate_proj.shape[1]
        shard_rows = query_proj.shape[0]

        shard_attn = jnp.concatenate(
            (query_proj, key_proj, value_proj, out_proj.reshape(shard_rows, -1)), 1
        )
        shard_mlp = jnp.concatenate((gate_proj, up_proj, pack_rows(down_proj, shard_rows)), 1)
        full_attn = lax.all_gather(shard_attn, "dp", axis=0, tiled=True)
        full_mlp = lax.all_gather(shard_mlp, "dp", axis=0, tiled=True)
        full_down = unpack_rows(full_mlp[:, 2 * units :], n_dp, width)
        if out_proj.shape == (shard_rows, width) and width_qkv % width == 0:
            out_source, out_column = full_attn, width_qkv // width
            full_out = full_attn[:, width_qkv:]
        else:
            full_out = full_attn[:, width_qkv:].reshape(-1, width)
            out_source, out_column = full_out, 0

        hidden_f = hidden_in.astype(F32)
        unit_attn, scale_attn = rms_unit(hidden_f)
        rows_hidden = sequence_rows(hidden_in)
        rows_attn = (rms_unit(rows_hidden.astype(F32))[0] * gain_attention).astype(BF)
        tables = rotary_tables(positions, HD)
        gains = (gain_query.reshape(1, HD), gain_key.reshape(1, HD))
        if paired:
            other_cot = swap(cotangent)
        else:
            rows_cot = lax.all_gather(cotangent, "tensor", axis=0, tiled=True)

        heads_b, *saved = attend(rows_attn, full_attn, tables, gains, groups_here, per_group)
        qraw, kraw, qb, kb, vb, lse = saved
        resid = hidden_f + scatter_rows(lambda h: matmul(h, full_out), heads_b)
        unit_mlp, scale_mlp = rms_unit(resid)
        normed_mlp = (unit_mlp * gain_feedforward).astype(BF)
        if paired:
            other_mlp = swap(normed_mlp)
            run = functools.partial(
                mlp, parts=2, full_mlp=full_mlp, full_down=full_down, units=units
            )
            *held, sent_down, sent_normed = run(other_mlp, other_cot, 1, dtype=BF)
            got_normed = swap(sent_normed)
            active_b, grad_gate_b, grad_up_b, own_down, own_normed = run(
                normed_mlp, cotangent, 0, dtype=F32, held=tuple(held)
            )
            grad_normed_mlp = own_normed + got_normed.astype(F32)
            rows_mlp = jnp.concatenate((normed_mlp, other_mlp), 0)
            rows_cot = jnp.concatenate((cotangent, other_cot), 0)
        else:
            rows_mlp = lax.all_gather(normed_mlp, "tensor", axis=0, tiled=True)
            active_b, grad_gate_b, grad_up_b, sent_down, sent_normed = mlp(
                rows_mlp, rows_cot, 0, 1, full_mlp, full_down, units, BF
            )
            grad_normed_mlp = sum_rows(sent_normed)
        grad_mlp_w = jnp.concatenate(
            (
                contract_rows(rows_mlp, grad_gate_b).astype(BF),
                contract_rows(rows_mlp, grad_up_b).astype(BF),
                pack_blocks(contract_rows(active_b, rows_cot).astype(BF), n_dp, shard_rows),
            ),
            1,
        )
        sent_mlp = lax.psum_scatter(grad_mlp_w, "dp", scatter_dimension=0, tiled=True)

        term_feedforward = jnp.sum(grad_normed_mlp * unit_mlp, 0)
        grad_resid = cotangent.astype(F32) + rms_back(
            grad_normed_mlp, gain_feedforward, unit_mlp, scale_mlp
        )
        rows_resid = sequence_rows(grad_resid.astype(BF))
        rows_resid, sent_down, grad_mlp_w = lax.optimization_barrier(
            (rows_resid, sent_down, grad_mlp_w)
        )
        if paired:
            output_b = (resid + own_down + swap(sent_down).astype(F32)).astype(BF)
        else:
            output_b = (resid + sum_rows(sent_down)).astype(BF)

        grad_qkv_b, terms_qk = attend_back(
            rows_resid,
            out_source,
            out_column,
            (qraw, kraw, qb, kb, vb, lse),
            tables,
            gains,
            groups_here,
            per_group,
        )
        grad_attn_w = jnp.concatenate(
            (
                contract_rows(rows_attn, grad_qkv_b).astype(BF),
                contract_rows(heads_b, rows_resid).astype(BF).reshape(width, -1),
            ),
            1,
        )
        grad_attn_w, sent_mlp = lax.optimization_barrier((grad_attn_w, sent_mlp))
        sent_attn = lax.psum_scatter(grad_attn_w, "dp", scatter_dimension=0, tiled=True)
        grad_normed_attn = scatter_rows(
            lambda g: contract_cols(g, full_attn[:, :width_qkv]), grad_qkv_b
        )
        term_attention = jnp.sum(grad_normed_attn * unit_attn, 0)
        grad_hidden = grad_resid + rms_back(
            grad_normed_attn, gain_attention, unit_attn, scale_attn
        )
        terms = all_sum(
            jnp.concatenate(
                (term_attention, term_feedforward, terms_qk[0], terms_qk[1])
            ).reshape(-1, HD),
            (("tensor", n_tensor), ("dp", n_dp)),
        ).reshape(-1)
        sent_attn = sent_attn.astype(F32)
        sent_mlp = sent_mlp.astype(F32)
        return (
            output_b,
            grad_hidden,
            terms[:width],
            terms[width : 2 * width],
            terms[2 * width : 2 * width + HD],
            terms[2 * width + HD :],
            sent_attn[:, :width_query],
            sent_attn[:, width_query : width_query + width_key],
            sent_attn[:, width_query + width_key : width_qkv],
            sent_attn[:, width_qkv:].reshape(out_proj.shape),
            sent_mlp[:, :units],
            sent_mlp[:, units : 2 * units],
            unpack_rows(sent_mlp[:, 2 * units :], 1, width),
        )

    return local


def solution(mesh):
    rows = P(("dp", "tensor"), None)
    cut = P("dp", "tensor")
    stacked = P(("tensor", "dp"), None)
    return jax.shard_map(
        make_local(mesh.shape["dp"], mesh.shape["tensor"]),
        mesh=mesh,
        in_specs=(
            rows,
            P("dp"),
            P(),
            P(),
            P(),
            P(),
            cut,
            cut,
            cut,
            stacked,
            cut,
            cut,
            stacked,
            rows,
        ),
        out_specs=(rows, rows, P(), P(), P(), P(), cut, cut, cut, stacked, cut, cut, stacked),
        check_vma=False,
    )
```

```python
import functools
import math

import jax
import jax.numpy as jnp
from jax import lax
from jax.experimental import pallas as pl
from jax.experimental.pallas import tpu as pltpu
from jax.sharding import PartitionSpec as P


HD = 128
EPS = 1e-06
THETA = 1000000.0
BF = jnp.bfloat16
F32 = jnp.float32


def rotary_tables(positions, width):
    half_width = width // 2
    freq_index = jnp.arange(half_width).astype(F32)
    inverse_freq = jnp.exp(freq_index * (-2.0 * math.log(THETA) / width))
    angles = positions.astype(F32)[:, None] * inverse_freq[None, :]
    cosine, sine = jnp.cos(angles), jnp.sin(angles)
    return jnp.concatenate((cosine, cosine), 1), jnp.concatenate((-sine, sine), 1)


def rms_unit(values):
    inv_scale = lax.rsqrt(jnp.mean(values * values, -1, keepdims=True) + EPS)
    return (values * inv_scale, inv_scale)


def rms_back(grad_out, gain_vec, unit_vals, inv_scale):
    scaled_grad = grad_out * gain_vec
    return inv_scale * (
        scaled_grad - unit_vals * jnp.mean(scaled_grad * unit_vals, -1, keepdims=True)
    )


def matmul(left, right):
    return jnp.dot(left, right, preferred_element_type=F32)


def contract_rows(left, right):
    return lax.dot_general(left, right, (((0,), (0,)), ((), ())), preferred_element_type=F32)


def contract_cols(left, right):
    return lax.dot_general(left, right, (((1,), (1,)), ((), ())), preferred_element_type=F32)


BLOCK = 256


def turn(values, cosine, sine):
    return values * cosine + pltpu.roll(values, HD // 2, 1) * sine


def turn_back(values, cosine, sine):
    return values * cosine - pltpu.roll(values, HD // 2, 1) * sine


def unit_of(raw):
    inv_scale = lax.rsqrt(jnp.mean(raw * raw, -1, keepdims=True) + EPS)
    return raw * inv_scale, inv_scale


def heads_stacked(ref, rows, per_group):
    return jnp.concatenate([ref[rows, r * HD : (r + 1) * HD] for r in range(per_group)], 0)


def causal_mask(key_end, row_start, block, per_group):
    keys = lax.broadcasted_iota(jnp.int32, (key_end, per_group * block), 0)
    queries = lax.broadcasted_iota(jnp.int32, (key_end, per_group * block), 1)
    return keys <= row_start + (queries & (block - 1))


def attend_kernel(
    x_ref,
    wq_ref,
    wk_ref,
    wv_ref,
    cos_ref,
    sin_ref,
    gq_ref,
    gk_ref,
    heads_ref,
    qraw_ref,
    kraw_ref,
    qb_ref,
    kb_ref,
    vb_ref,
    lse_ref,
    *,
    per_group,
    block,
):
    length = x_ref.shape[0]
    scale_qk = 1.0 / math.sqrt(HD)
    for i in range(length // block):
        rows = slice(i * block, (i + 1) * block)
        x = x_ref[rows, :]
        cosine, sine = cos_ref[rows, :], sin_ref[rows, :]
        qraw = jnp.dot(x, wq_ref[...], preferred_element_type=F32)
        kraw = jnp.dot(x, wk_ref[...], preferred_element_type=F32)
        qraw_ref[rows, :] = qraw
        kraw_ref[rows, :] = kraw
        vb_ref[rows, :] = jnp.dot(x, wv_ref[...], preferred_element_type=F32).astype(BF)
        for r in range(per_group):
            cols = slice(r * HD, (r + 1) * HD)
            unit, _ = unit_of(qraw[:, cols])
            qb_ref[rows, cols] = turn(unit * gq_ref[...], cosine, sine).astype(BF)
        unit, _ = unit_of(kraw)
        kb_ref[rows, :] = turn(unit * gk_ref[...], cosine, sine).astype(BF)
        key_end = (i + 1) * block
        queries = heads_stacked(qb_ref, rows, per_group)
        scores = contract_cols(kb_ref[:key_end, :], queries) * scale_qk
        scores = jnp.where(causal_mask(key_end, i * block, block, per_group), scores, -jnp.inf)
        top = jnp.max(scores, 0, keepdims=True)
        shifted = jnp.exp(scores - top)
        total = jnp.sum(shifted, 0, keepdims=True)
        probs = (shifted * (1.0 / total)).astype(BF)
        out = contract_rows(vb_ref[:key_end, :], probs).T
        log_sum = top + jnp.log(total)
        for r in range(per_group):
            part = slice(r * block, (r + 1) * block)
            heads_ref[rows, r * HD : (r + 1) * HD] = out[part, :].astype(BF)
            lse_ref[r : r + 1, rows] = log_sum[:, part]


def attend_back_kernel(
    resid_ref,
    wo_ref,
    qb_ref,
    kb_ref,
    vb_ref,
    qraw_ref,
    kraw_ref,
    lse_ref,
    cos_ref,
    sin_ref,
    gq_ref,
    gk_ref,
    grad_ref,
    term_ref,
    key_acc,
    value_acc,
    *,
    per_group,
    block,
    groups,
):
    length = resid_ref.shape[0]
    scale_qk = 1.0 / math.sqrt(HD)
    group = pl.program_id(0)
    blocks = length // block

    @pl.when(group == 0)
    def _():
        term_ref[...] = jnp.zeros_like(term_ref)

    def column(index):
        return pl.ds(pl.multiple_of(index * HD, HD), HD)

    for i in reversed(range(blocks)):
        rows = slice(i * block, (i + 1) * block)
        key_end = (i + 1) * block
        grad = contract_cols(resid_ref[rows, :], wo_ref[...]).astype(BF)
        grads = jnp.concatenate(
            [grad[:, r * HD : (r + 1) * HD] for r in range(per_group)], 0
        )
        queries = heads_stacked(qb_ref, rows, per_group)
        keys, values = kb_ref[:key_end, :], vb_ref[:key_end, :]
        log_sum = jnp.concatenate([lse_ref[r : r + 1, rows] for r in range(per_group)], 1)
        scores = contract_cols(keys, queries) * scale_qk
        probs = jnp.where(
            causal_mask(key_end, i * block, block, per_group), jnp.exp(scores - log_sum), 0.0
        )
        grad_probs = contract_cols(values, grads)
        row_dot = jnp.sum(probs * grad_probs, 0, keepdims=True)
        grad_scores = (probs * (grad_probs - row_dot)).astype(BF)
        value_part = jnp.dot(probs.astype(BF), grads, preferred_element_type=F32)
        key_part = jnp.dot(grad_scores, queries, preferred_element_type=F32) * scale_qk
        if i == blocks - 1:
            value_acc[...] = value_part
            key_acc[...] = key_part
        else:
            value_acc[:key_end, :] += value_part
            key_acc[:key_end, :] += key_part
        grad_query = contract_rows(keys, grad_scores).T * scale_qk
        cosine, sine = cos_ref[rows, :], sin_ref[rows, :]
        for r in range(per_group):
            normed = turn_back(grad_query[r * block : (r + 1) * block, :], cosine, sine)
            unit, inv_scale = unit_of(qraw_ref[rows, r * HD : (r + 1) * HD])
            term_ref[0:1, :] += jnp.sum(normed * unit, 0, keepdims=True)
            grad_ref[rows, column(group * per_group + r)] = rms_back(
                normed, gq_ref[...], unit, inv_scale
            ).astype(BF)
    for i in range(blocks):
        rows = slice(i * block, (i + 1) * block)
        normed = turn_back(key_acc[rows, :], cos_ref[rows, :], sin_ref[rows, :])
        unit, inv_scale = unit_of(kraw_ref[rows, :])
        term_ref[1:2, :] += jnp.sum(normed * unit, 0, keepdims=True)
        grad_ref[rows, column(groups * per_group + group)] = rms_back(
            normed, gk_ref[...], unit, inv_scale
        ).astype(BF)
        grad_ref[rows, column(groups * (per_group + 1) + group)] = value_acc[rows, :].astype(BF)


def attend(rows_attn, full_attn, tables, gains, groups, per_group):
    length, width = rows_attn.shape
    block = min(length, BLOCK)
    heads = groups * per_group
    whole = lambda shape: pl.BlockSpec(shape, lambda g: (0, 0))
    wide = pl.BlockSpec((length, per_group * HD), lambda g: (0, g))
    narrow = pl.BlockSpec((length, HD), lambda g: (0, g))
    return pl.pallas_call(
        functools.partial(attend_kernel, per_group=per_group, block=block),
        name="attend",
        grid=(groups,),
        in_specs=[
            whole((length, width)),
            pl.BlockSpec((width, per_group * HD), lambda g: (0, g)),
            pl.BlockSpec((width, HD), lambda g: (0, heads + g)),
            pl.BlockSpec((width, HD), lambda g: (0, heads + groups + g)),
            whole((length, HD)),
            whole((length, HD)),
            whole((1, HD)),
            whole((1, HD)),
        ],
        out_specs=[
            wide,
            wide,
            narrow,
            wide,
            narrow,
            narrow,
            pl.BlockSpec((None, per_group, length), lambda g: (g, 0, 0)),
        ],
        out_shape=[
            jax.ShapeDtypeStruct((length, heads * HD), BF),
            jax.ShapeDtypeStruct((length, heads * HD), F32),
            jax.ShapeDtypeStruct((length, groups * HD), F32),
            jax.ShapeDtypeStruct((length, heads * HD), BF),
            jax.ShapeDtypeStruct((length, groups * HD), BF),
            jax.ShapeDtypeStruct((length, groups * HD), BF),
            jax.ShapeDtypeStruct((groups, per_group, length), F32),
        ],
        cost_estimate=pl.CostEstimate(
            flops=2 * length * width * (heads + 2 * groups) * HD + 3 * length * length * heads * HD,
            bytes_accessed=length * (heads + 2 * groups) * HD * 10,
            transcendentals=length * length * heads,
        ),
    )(rows_attn, full_attn, full_attn, full_attn, *tables, *gains)


def attend_back(
    rows_resid, full_out, out_column, saved, tables, gains, groups, per_group, first, count
):
    length, width = rows_resid.shape
    qraw, kraw, qb, kb, vb, lse = saved
    block = min(length, BLOCK)
    columns = count * (per_group + 2) * HD
    whole = lambda shape: pl.BlockSpec(shape, lambda g: (0, 0))
    wide = pl.BlockSpec((length, per_group * HD), lambda g: (0, first + g))
    narrow = pl.BlockSpec((length, HD), lambda g: (0, first + g))
    return pl.pallas_call(
        functools.partial(attend_back_kernel, per_group=per_group, block=block, groups=count),
        name="attend_back",
        grid=(count,),
        in_specs=[
            whole((length, width)),
            pl.BlockSpec((per_group * HD, width), lambda g: (first + g, out_column)),
            wide,
            narrow,
            narrow,
            wide,
            narrow,
            pl.BlockSpec((None, per_group, length), lambda g: (first + g, 0, 0)),
            whole((length, HD)),
            whole((length, HD)),
            whole((1, HD)),
            whole((1, HD)),
        ],
        out_specs=[whole((length, columns)), whole((8, HD))],
        out_shape=[
            jax.ShapeDtypeStruct((length, columns), BF),
            jax.ShapeDtypeStruct((8, HD), F32),
        ],
        scratch_shapes=[pltpu.VMEM((length, HD), F32), pltpu.VMEM((length, HD), F32)],
        cost_estimate=pl.CostEstimate(
            flops=(2 * width + 7 * length) * length * count * per_group * HD,
            bytes_accessed=length * columns * 10,
            transcendentals=length * length * count * per_group,
        ),
    )(rows_resid, full_out, qb, kb, vb, qraw, kraw, lse, *tables, *gains)


def mlp_kernel(
    x_ref,
    cot_ref,
    wg_ref,
    wu_ref,
    wd_ref,
    *refs,
    steps,
):
    active_ref, gate_ref, up_ref, down_ref, normed_ref, down_acc, normed_acc = refs[-7:]
    step = pl.program_id(0)

    @pl.when(step == 0)
    def _():
        down_acc[...] = jnp.zeros_like(down_acc)
        normed_acc[...] = jnp.zeros_like(normed_acc)

    half = min(x_ref.shape[0], 256)
    for i in range(x_ref.shape[0] // half):
        rows = slice(i * half, (i + 1) * half)
        x = x_ref[rows, :]
        gate = jnp.dot(x, wg_ref[...], preferred_element_type=F32)
        up = jnp.dot(x, wu_ref[...], preferred_element_type=F32)
        grad_active = contract_cols(cot_ref[rows, :], wd_ref[...])
        sigmoid = 1.0 / (1.0 + jnp.exp(-gate))
        silu = gate * sigmoid
        active = (silu * up).astype(BF)
        grad_gate = (grad_active * up * sigmoid * (1.0 + gate * (1.0 - sigmoid))).astype(BF)
        grad_up = (grad_active * silu).astype(BF)
        active_ref[rows, :] = active
        gate_ref[rows, :] = grad_gate
        up_ref[rows, :] = grad_up
        down_acc[rows, :] += jnp.dot(active, wd_ref[...], preferred_element_type=F32)
        normed_acc[rows, :] += contract_cols(grad_gate, wg_ref[...]) + contract_cols(
            grad_up, wu_ref[...]
        )

    @pl.when(step == steps - 1)
    def _():
        down_ref[...] = down_acc[...].astype(down_ref.dtype)
        normed_ref[...] = normed_acc[...].astype(normed_ref.dtype)


def mlp(rows_x, rows_cot, part, parts, full_mlp, full_down, units, dtype, held=()):
    rows, width = rows_x.shape
    block = next(b for b in (512, 384, 256, 128) if units % b == 0)
    steps = units // block
    whole = pl.BlockSpec((rows, width), lambda j: (0, 0))
    piece = pl.BlockSpec((rows, block), lambda j: (part, j))
    full = jax.ShapeDtypeStruct((rows * parts, units), BF)
    total = jax.ShapeDtypeStruct((rows, width), dtype)
    return pl.pallas_call(
        functools.partial(mlp_kernel, steps=steps),
        name="feed_forward",
        grid=(steps,),
        in_specs=[
            whole,
            whole,
            pl.BlockSpec((width, block), lambda j: (0, j)),
            pl.BlockSpec((width, block), lambda j: (0, steps + j)),
            pl.BlockSpec((block, width), lambda j: (j, 0)),
        ]
        + [pl.BlockSpec(memory_space=pl.ANY)] * len(held),
        out_specs=[piece, piece, piece, whole, whole],
        out_shape=[full, full, full, total, total],
        input_output_aliases={5 + i: i for i in range(len(held))},
        scratch_shapes=[pltpu.VMEM((rows, width), F32), pltpu.VMEM((rows, width), F32)],
        cost_estimate=pl.CostEstimate(
            flops=12 * rows * width * units,
            bytes_accessed=6 * width * units + 6 * rows * units,
            transcendentals=rows * units,
        ),
    )(rows_x, rows_cot, full_mlp, full_mlp, full_down, *held)


def all_sum(value, sizes):
    for axis, size in sizes:
        if size & (size - 1):
            value = lax.psum(value, axis)
            continue
        step = 1
        while step < size:
            value = value + lax.ppermute(value, axis, [(i, i ^ step) for i in range(size)])
            step *= 2
    return value


def pick(array, index, axis):
    return lax.dynamic_index_in_dim(array, index, axis, keepdims=False)


def near_stages(value, n_dp):
    me = lax.axis_index("dp")
    blocks = value.reshape(n_dp // 4, 2, 2, -1, value.shape[-1])
    for bit, step, axis in ((me % 2, 1, 2), (me // 2 % 2, 2, 1)):
        sent = pick(blocks, 1 - bit, axis)
        got = yield (lax.ppermute(sent, "dp", [(i, i ^ step) for i in range(n_dp)]),)
        blocks = pick(blocks, bit, axis) + got[0]
    yield (blocks,)


def line_stages(blocks, n_dp):
    depth = n_dp // 4
    level = lax.axis_index("dp") // 4
    up = down = None
    for step in range(1, depth):
        send_up = pick(blocks, jnp.minimum(level + depth - step, depth - 1), 0)
        send_down = pick(blocks, jnp.maximum(level - depth + step, 0), 0)
        if step > 1:
            send_up, send_down = send_up + up, send_down + down
        up, down = yield (
            lax.ppermute(send_up, "dp", [(i, i + 4) for i in range(4 * step)]),
            lax.ppermute(send_down, "dp", [(i, i - 4) for i in range(n_dp - 4 * step, n_dp)]),
        )
    total = pick(blocks, level, 0).astype(F32)
    if depth > 1:
        total = total + up.astype(F32) + down.astype(F32)
    yield (total,)


def sum_stages(value, sizes):
    for axis, size in sizes:
        step = 1
        while step < size:
            got = yield (lax.ppermute(value, axis, [(i, i ^ step) for i in range(size)]),)
            value = value + got[0]
            step *= 2
    yield (value,)


class Waves:
    def __init__(self, lengths):
        self.lengths, self.chains, self.held, self.sums = lengths, {}, {}, {}

    def add(self, name, chain):
        self.chains[name] = chain
        self.held[name] = next(chain)

    def advance(self, *beside, only=None):
        names = list(self.held) if only is None else [only]
        values = [self.held.pop(n) for n in names]
        if only is None:
            values, beside = lax.optimization_barrier((values, beside))
        for name, value in zip(names, values):
            self.lengths[name] -= 1
            got = self.chains[name].send(value)
            if self.lengths[name]:
                self.held[name] = got
            else:
                self.sums[name] = got[0]
        return beside


def pack_rows(shard, rows):
    count, width = shard.shape
    if 2 * count == 3 * rows and rows % 32 == 0:
        tail = shard[rows:]
        half = width // 2
        return jnp.concatenate(
            (shard[:rows], jnp.concatenate((tail[:, :half], tail[:, half:]), 0)), 1
        )
    return shard.reshape(rows, -1)


def unpack_rows(packed, parts, width):
    total, wide = packed.shape
    rows = total // parts
    if 2 * wide == 3 * width and rows % 32 == 0:
        blocks = packed.reshape(parts, rows, wide)
        tail = blocks[:, :, width:]
        tail = jnp.concatenate((tail[:, : rows // 2], tail[:, rows // 2 :]), 2)
        return jnp.concatenate((blocks[:, :, :width], tail), 1).reshape(-1, width)
    return packed.reshape(-1, width)


def pack_blocks(full, parts, rows):
    total, width = full.shape
    count = total // parts
    if 2 * count == 3 * rows and rows % 32 == 0:
        blocks = full.reshape(parts, count, width)
        tail = blocks[:, rows:]
        half = width // 2
        tail = jnp.concatenate((tail[:, :, :half], tail[:, :, half:]), 1)
        return jnp.concatenate((blocks[:, :rows], tail), 2).reshape(parts * rows, -1)
    return full.reshape(parts * rows, -1)


def make_local(n_dp, n_tensor):
    paired = n_tensor == 2

    def swap(value):
        return lax.ppermute(value, "tensor", [(0, 1), (1, 0)])

    def in_order(own, other):
        first = lax.axis_index("tensor") == 0
        return jnp.concatenate((jnp.where(first, own, other), jnp.where(first, other, own)), 0)

    def sequence_rows(own):
        if paired:
            return in_order(own, swap(own))
        return lax.all_gather(own, "tensor", axis=0, tiled=True)

    def scatter_rows(part, operand):
        if paired:
            half = operand.shape[0] // 2
            me = lax.axis_index("tensor")
            other_rows = lax.dynamic_slice_in_dim(operand, (1 - me) * half, half, 0)
            own_rows = lax.dynamic_slice_in_dim(operand, me * half, half, 0)
            got = swap(part(other_rows).astype(BF))
            return part(own_rows) + got.astype(F32)
        return sum_rows(part(operand).astype(BF))

    def sum_rows(value):
        return lax.psum_scatter(value, "tensor", scatter_dimension=0, tiled=True).astype(F32)

    def local(
        hidden_in,
        positions,
        gain_attention,
        gain_feedforward,
        gain_query,
        gain_key,
        query_proj,
        key_proj,
        value_proj,
        out_proj,
        gate_proj,
        up_proj,
        down_proj,
        cotangent,
    ):
        width = hidden_in.shape[1]
        heads_here = query_proj.shape[1] // HD
        groups_here = key_proj.shape[1] // HD
        per_group = heads_here // groups_here
        width_query = heads_here * HD
        width_key = groups_here * HD
        width_qkv = width_query + 2 * width_key
        units = gate_proj.shape[1]
        shard_rows = query_proj.shape[0]

        shard_attn = jnp.concatenate(
            (query_proj, key_proj, value_proj, out_proj.reshape(shard_rows, -1)), 1
        )
        shard_mlp = jnp.concatenate((gate_proj, up_proj, pack_rows(down_proj, shard_rows)), 1)
        full_attn = lax.all_gather(shard_attn, "dp", axis=0, tiled=True)
        full_mlp = lax.all_gather(shard_mlp, "dp", axis=0, tiled=True)
        full_down = unpack_rows(full_mlp[:, 2 * units :], n_dp, width)
        if out_proj.shape == (shard_rows, width) and width_qkv % width == 0:
            out_source, out_column = full_attn, width_qkv // width
            full_out = full_attn[:, width_qkv:]
        else:
            full_out = full_attn[:, width_qkv:].reshape(-1, width)
            out_source, out_column = full_out, 0

        hidden_f = hidden_in.astype(F32)
        unit_attn, scale_attn = rms_unit(hidden_f)
        rows_hidden = sequence_rows(hidden_in)
        unit_rows = rms_unit(rows_hidden.astype(F32))[0]
        rows_attn = (unit_rows * gain_attention).astype(BF)
        if paired:
            other_cot = swap(cotangent)
            rows_attn, other_cot = lax.optimization_barrier((rows_attn, other_cot))
        else:
            rows_cot = lax.all_gather(cotangent, "tensor", axis=0, tiled=True)
        tables = rotary_tables(positions, HD)
        gains = (gain_query.reshape(1, HD), gain_key.reshape(1, HD))
        heads_b, *saved = attend(rows_attn, full_attn, tables, gains, groups_here, per_group)
        qraw, kraw, qb, kb, vb, lse = saved
        resid = hidden_f + scatter_rows(lambda h: matmul(h, full_out), heads_b)
        unit_mlp, scale_mlp = rms_unit(resid)
        normed_mlp = (unit_mlp * gain_feedforward).astype(BF)
        if paired:
            other_mlp = swap(normed_mlp)
            run = functools.partial(
                mlp, parts=2, full_mlp=full_mlp, full_down=full_down, units=units
            )
            *held, sent_down, sent_normed = run(other_mlp, other_cot, 1, dtype=BF)
            got_normed = swap(sent_normed)
            active_b, grad_gate_b, grad_up_b, own_down, own_normed = run(
                normed_mlp, cotangent, 0, dtype=F32, held=tuple(held)
            )
            grad_normed_mlp = own_normed + got_normed.astype(F32)
            rows_mlp = jnp.concatenate((normed_mlp, other_mlp), 0)
            rows_cot = jnp.concatenate((cotangent, other_cot), 0)
        else:
            rows_mlp = lax.all_gather(normed_mlp, "tensor", axis=0, tiled=True)
            active_b, grad_gate_b, grad_up_b, sent_down, sent_normed = mlp(
                rows_mlp, rows_cot, 0, 1, full_mlp, full_down, units, BF
            )
            grad_normed_mlp = sum_rows(sent_normed)
        grad_mlp_w = jnp.concatenate(
            (
                contract_rows(rows_mlp, grad_gate_b).astype(BF),
                contract_rows(rows_mlp, grad_up_b).astype(BF),
                pack_blocks(contract_rows(active_b, rows_cot).astype(BF), n_dp, shard_rows),
            ),
            1,
        )
        sent_mlp = lax.psum_scatter(grad_mlp_w, "dp", scatter_dimension=0, tiled=True)

        term_feedforward = jnp.sum(grad_normed_mlp * unit_mlp, 0)
        grad_resid = cotangent.astype(F32) + rms_back(
            grad_normed_mlp, gain_feedforward, unit_mlp, scale_mlp
        )
        rows_resid = sequence_rows(grad_resid.astype(BF))
        rows_resid, sent_down, grad_mlp_w = lax.optimization_barrier(
            (rows_resid, sent_down, grad_mlp_w)
        )
        if paired:
            output_b = (resid + own_down + swap(sent_down).astype(F32)).astype(BF)
        else:
            output_b = (resid + sum_rows(sent_down)).astype(BF)

        back = functools.partial(
            attend_back,
            full_out=out_source,
            out_column=out_column,
            saved=(qraw, kraw, qb, kb, vb, lse),
            tables=tables,
            gains=gains,
            groups=groups_here,
            per_group=per_group,
        )
        wide, narrow = width_query // 2, width_key // 2
        sizes = (("tensor", n_tensor), ("dp", n_dp))
        if paired and n_dp % 4 == 0 and groups_here % 2 == 0 and n_dp & (n_dp - 1) == 0:
            waves = Waves(
                {"out": 2, "a": 2, "b": 2, "line": n_dp // 4 - 1, "terms": n_dp.bit_length()}
            )
            half = groups_here // 2
            waves.add("out", near_stages(contract_rows(heads_b, rows_resid).astype(BF), n_dp))
            grads_a, terms_a = back(rows_resid, first=0, count=half)
            (rows_a,) = waves.advance(grads_a)
            waves.add("a", near_stages(contract_rows(rows_attn, rows_a).astype(BF), n_dp))
            grads_b, terms_b = back(rows_resid, first=half, count=half)
            (rows_b,) = waves.advance(grads_b)
            waves.add("b", near_stages(contract_rows(rows_attn, rows_b).astype(BF), n_dp))
            waves.advance(only="b")

            def part(g_a, g_b):
                total = contract_cols(g_a[:, :wide], full_attn[:, :wide])
                total += contract_cols(g_b[:, :wide], full_attn[:, wide:width_query])
                for k in range(2):
                    at = width_query + k * width_key
                    to = wide + k * narrow
                    total += contract_cols(
                        g_a[:, to : to + narrow], full_attn[:, at : at + narrow]
                    )
                    total += contract_cols(
                        g_b[:, to : to + narrow], full_attn[:, at + narrow : at + width_key]
                    )
                return total

            me = lax.axis_index("tensor")
            rows = rows_attn.shape[0] // 2

            def take(array, index):
                return lax.dynamic_slice_in_dim(array, index * rows, rows, 0)

            other = part(take(rows_a, 1 - me), take(rows_b, 1 - me))
            got = swap(other.astype(BF))
            mine = part(take(rows_a, me), take(rows_b, me))
            term_attention = jnp.sum(other * take(unit_rows, 1 - me), 0) + jnp.sum(
                mine * unit_attn, 0
            )
            terms_qk = terms_a + terms_b
            all_terms = jnp.concatenate(
                (term_attention, term_feedforward, terms_qk[0], terms_qk[1])
            ).reshape(-1, HD)
            waves.add("terms", sum_stages(all_terms, sizes[::-1]))
            waves.advance()
            near = jnp.concatenate([waves.sums[n] for n in ("out", "a", "b")], -1)
            waves.add("line", line_stages(near, n_dp))
            while waves.held:
                waves.advance()
            grad_normed_attn = mine + got.astype(F32)
            line, cut = waves.sums["line"], wide + 2 * narrow
            sent_out, sent_a = line[:, :width], line[:, width : width + cut]
            sent_b = line[:, width + cut :]
            terms = waves.sums["terms"].reshape(-1)
            sent_q = jnp.concatenate((sent_a[:, :wide], sent_b[:, :wide]), 1)
            sent_k = jnp.concatenate(
                (sent_a[:, wide : wide + narrow], sent_b[:, wide : wide + narrow]), 1
            )
            sent_v = jnp.concatenate((sent_a[:, wide + narrow :], sent_b[:, wide + narrow :]), 1)
        else:
            grad_qkv_b, terms_qk = back(rows_resid, first=0, count=groups_here)
            grad_attn_w = jnp.concatenate(
                (
                    contract_rows(rows_attn, grad_qkv_b).astype(BF),
                    contract_rows(heads_b, rows_resid).astype(BF).reshape(width, -1),
                ),
                1,
            )
            sent_attn = lax.psum_scatter(
                grad_attn_w, "dp", scatter_dimension=0, tiled=True
            ).astype(F32)
            sent_q = sent_attn[:, :width_query]
            sent_k = sent_attn[:, width_query : width_query + width_key]
            sent_v = sent_attn[:, width_query + width_key : width_qkv]
            sent_out = sent_attn[:, width_qkv:].reshape(out_proj.shape)
            grad_normed_attn = scatter_rows(
                lambda g: contract_cols(g, full_attn[:, :width_qkv]), grad_qkv_b
            )
            term_attention = jnp.sum(grad_normed_attn * unit_attn, 0)
            terms = all_sum(
                jnp.concatenate(
                    (term_attention, term_feedforward, terms_qk[0], terms_qk[1])
                ).reshape(-1, HD),
                sizes,
            ).reshape(-1)
        grad_hidden = grad_resid + rms_back(
            grad_normed_attn, gain_attention, unit_attn, scale_attn
        )
        sent_mlp = sent_mlp.astype(F32)
        return (
            output_b,
            grad_hidden,
            terms[:width],
            terms[width : 2 * width],
            terms[2 * width : 2 * width + HD],
            terms[2 * width + HD :],
            sent_q,
            sent_k,
            sent_v,
            sent_out,
            sent_mlp[:, :units],
            sent_mlp[:, units : 2 * units],
            unpack_rows(sent_mlp[:, 2 * units :], 1, width),
        )

    return local


def solution(mesh):
    rows = P(("dp", "tensor"), None)
    cut = P("dp", "tensor")
    stacked = P(("tensor", "dp"), None)
    local = make_local(mesh.shape["dp"], mesh.shape["tensor"])

    return jax.shard_map(
        local,
        mesh=mesh,
        in_specs=(
            rows,
            P("dp"),
            P(),
            P(),
            P(),
            P(),
            cut,
            cut,
            cut,
            stacked,
            cut,
            cut,
            stacked,
            rows,
        ),
        out_specs=(rows, rows, P(), P(), P(), P(), cut, cut, cut, stacked, cut, cut, stacked),
        check_vma=False,
    )
```
